32 devices in a mesh: gx: 2 (over core), gy: 4 (over y, x), gz: 4 (over z).
Axes of the slice: x: 2, y: 2, z: 4, core: 2. Of those that a mesh axis runs over, the one named last changes fastest.
Arguments:
- right_side: float32 [96, 192, 192], P('gx', 'gy', 'gz'), may hold values from -6 to 6
- start_guess: float32 [96, 192, 192], P('gx', 'gy', 'gz'), may hold values from -3 to 3
- reaction: float32 [96, 192, 192], P('gx', 'gy', 'gz'), may hold values from 0.0005 to 0.005
Outputs:
- solution_field: float32 [96, 192, 192], P('gx', 'gy', 'gz')
- residual: float32 [96, 192, 192], P('gx', 'gy', 'gz')
The draws below stay inside these ranges and needn't reach their ends.
All inputs are finite; a program needn't handle non-finite values.
Results may differ from the reference program's by a relative error of at most 0.0003.
Values sent between devices are 32-bit elements.
A program may use at most 128 MiB of HBM per device.

```python
import math
import jax
import jax.numpy as jnp

LEVELS = 5
BOTTOM_ITERS = 6
NX = 96
NY = 192
NZ = 192


def block_scale(rng, shape, cuts, low, largest):
    def one(axis_at, parts):
        heights = jax.random.uniform(jax.random.fold_in(jax.random.fold_in(rng, 6), axis_at), (parts,), jnp.float32, low / len(cuts), largest / len(cuts))
        return jnp.repeat(jnp.exp(heights), shape[axis_at] // parts).reshape((-1,) + (1,) * (len(shape) - axis_at - 1))

    gain = one(*cuts[0])
    for cut in cuts[1:]:
        gain = gain * one(*cut)
    return gain


def scatter_about(own_key, extent, scale, bound, shards=(), dtype=jnp.bfloat16):
    values = jax.random.normal(own_key, extent, jnp.float32) * scale
    if len(shards) > 0:
        values = block_scale(own_key, extent, shards, -0.22, 0.18) * values
    return jnp.clip(values, min=-bound, max=bound).astype(dtype)


def setup_inputs(seed: int = 0) -> dict:
    key_list = jax.random.split(jax.random.key(seed), 4)
    right_side = scatter_about(key_list[0], (NX, NY, NZ), 1.0, 6.0, ((0, 2), (1, 4), (2, 4)), jnp.float32)
    start_guess = scatter_about(key_list[1], (NX, NY, NZ), 0.2, 3.0, ((0, 2), (1, 4), (2, 4)), jnp.float32)
    reaction = jnp.clip(jnp.exp(math.log(0.005) - 2.30258502 * jax.random.uniform(key_list[2], (NX, NY, NZ), jnp.float32) ** block_scale(key_list[2], (NX, NY, NZ), ((0, 2), (1, 4), (2, 4)), -0.2, 0.2)), 0.0005, 0.005)
    return {"right_side": right_side, "start_guess": start_guess, "reaction": reaction}


damping = 6.0 / 7.0


def operate(values, shifted, factor):
    padded = jnp.pad(values, 1)
    beside = padded[2:, 1:-1, 1:-1] + padded[:-2, 1:-1, 1:-1]
    beside = beside + padded[1:-1, 2:, 1:-1] + padded[1:-1, :-2, 1:-1]
    beside = beside + padded[1:-1, 1:-1, 2:] + padded[1:-1, 1:-1, :-2]
    return factor * (6.0 * values - beside) + shifted * values


def coarsen(values):
    size_x, size_y, size_z = values.shape
    blocks = values.reshape(size_x // 2, 2, size_y // 2, 2, size_z // 2, 2)
    return jnp.mean(blocks, axis=(1, 3, 5))


def refine(values):
    size_x, size_y, size_z = values.shape
    spread = jnp.broadcast_to(values[:, None, :, None, :, None], (size_x, 2, size_y, 2, size_z, 2))
    return spread.reshape(2 * size_x, 2 * size_y, 2 * size_z)


def smooth_once(estimate, source, shifted, factor):
    return estimate + damping * (source - operate(estimate, shifted, factor)) / (6.0 * factor + shifted)


def bottom(source, shifted, factor):
    estimate = jnp.zeros_like(source)
    leftover = source
    direction = source
    norm_now = jnp.sum(leftover * leftover)
    for repeat_index in range(BOTTOM_ITERS):
        applied = operate(direction, shifted, factor)
        step_length = norm_now / jnp.sum(direction * applied)
        estimate = estimate + step_length * direction
        leftover = leftover - step_length * applied
        norm_next = jnp.sum(leftover * leftover)
        direction = leftover + (norm_next / norm_now) * direction
        norm_now = norm_next
    return estimate


def vcycle_level(source, shifts, depth_index):
    factor = 0.25 ** depth_index
    shifted = shifts[depth_index]
    if depth_index == LEVELS - 1:
        return bottom(source, shifted, factor)
    estimate = damping * source / (6.0 * factor + shifted)
    estimate = smooth_once(estimate, source, shifted, factor)
    leftover = source - operate(estimate, shifted, factor)
    estimate = estimate + refine(vcycle_level(coarsen(leftover), shifts, depth_index + 1))
    estimate = smooth_once(estimate, source, shifted, factor)
    estimate = smooth_once(estimate, source, shifted, factor)
    return estimate


def reference(right_side, start_guess, reaction):
    shifts = [reaction]
    for depth_index in range(LEVELS - 1):
        shifts.append(coarsen(shifts[-1]))
    start_residual = right_side - operate(start_guess, reaction, 1.0)
    precond = vcycle_level(start_residual, shifts, 0)
    upper = jnp.sum(start_residual * precond)
    applied = operate(precond, reaction, 1.0)
    step_length = upper / jnp.sum(precond * applied)
    solution_field = start_guess + step_length * precond
    residual = start_residual - step_length * applied
    return solution_field, residual
```

```python
import jax
import jax.numpy as jnp
from jax import lax
from jax.experimental import pallas as pl
from jax.experimental.pallas import tpu as pltpu
from jax.sharding import PartitionSpec as P

LEVELS = 5
BOTTOM_ITERS = 6
LOCAL = 2
AXES = ("gx", "gy", "gz")
MESH = pl.DeviceIdType.MESH
F32 = jnp.float32

damping = 6.0 / 7.0


def up_to(n, m):
    return -(-n // m) * m


def lanes_of(shape):
    return up_to(max(shape[2] + 1, shape[0]), 128)


def halved(shape, times):
    return tuple(s >> times for s in shape)


def loop(n, f, carry=0, unroll=4):
    while n % unroll:
        unroll -= 1

    def step(i, c):
        for k in range(unroll):
            c = f(i * unroll + k, c)
        return c

    return lax.fori_loop(0, n // unroll, step, carry)


def lane_of(rows, lanes):
    return lax.broadcasted_iota(jnp.int32, (rows, lanes), 1)


def pick(lanes_in, lanes_out, f, value):
    r = lax.broadcasted_iota(jnp.int32, (lanes_in, lanes_out), 0)
    c = lax.broadcasted_iota(jnp.int32, (lanes_in, lanes_out), 1)
    return jnp.where(f(r, c), value, 0.0).astype(F32)


def dot(a, b):
    return lax.dot(a, b, precision=lax.Precision.HIGHEST, preferred_element_type=F32)


def total(v):
    v = jnp.sum(v, axis=0, keepdims=True)
    return jnp.sum(v, axis=1, keepdims=True)


def fold(v):
    out = v[0:8]
    for k in range(1, v.shape[0] // 8):
        out = out + v[8 * k : 8 * k + 8]
    return out


def make_kernel(sizes, block):
    nx, ny, nz = sizes
    whole = (block[0] * nx, block[1] * ny, block[2] * nz)
    shapes = [halved(block, k) if k < LOCAL else halved(whole, k) for k in range(LEVELS)]
    lanes = [lanes_of(s) for s in shapes]
    counts = [6, 4]
    part = halved(block, LOCAL)
    wide = shapes[LOCAL][2]
    packs = 2 if wide <= 64 and part[0] % 2 == 0 else 1
    slabs = part[0] // packs
    rows = up_to(part[1], 8)
    glanes = lanes[LOCAL]
    half = glanes // packs

    scratch = {}
    for k in range(LEVELS):
        X, Y, Z = shapes[k]
        L = lanes[k]
        Yp = up_to(Y, 8)
        n = counts[k] if k < LOCAL else 2
        scratch[f"e{k}"] = pltpu.VMEM((n, X + 2, Yp + 16, L), F32)
        scratch[f"f{k}"] = pltpu.VMEM((X, Yp, L), F32)
        scratch[f"s{k}"] = pltpu.VMEM((X, Yp, L), F32)
        scratch[f"w{k}"] = pltpu.VMEM((X, Yp, L), F32)
        if k < LEVELS - 1:
            scratch[f"t{k}"] = pltpu.VMEM((L // 128, X // 2, 2 * up_to(Y // 2, 8), 128), F32)
        if k < LOCAL:
            for name, n_rows in (("zs", Y), ("zr", Y), ("ys", X), ("yr", X)):
                scratch[f"{name}{k}"] = pltpu.VMEM((n, 2, n_rows, L), F32)
            scratch[f"send{k}"] = pltpu.SemaphoreType.DMA((n, 6))
            scratch[f"recv{k}"] = pltpu.SemaphoreType.DMA((n, 6))
    scratch["ap"] = pltpu.VMEM((block[0], block[1], lanes[0]), F32)
    for g in range(2):
        scratch[f"gz{g}"] = pltpu.VMEM((nz, slabs, rows, glanes), F32)
        scratch[f"gm{g}"] = pltpu.VMEM((slabs, rows, glanes), F32)
        scratch[f"gy{g}"] = pltpu.VMEM((slabs, ny * rows, glanes), F32)
        scratch[f"gx{g}"] = pltpu.VMEM((nx, slabs, ny * rows, glanes), F32)
    for i, n in enumerate(sizes):
        scratch[f"q{i}"] = pltpu.VMEM((n, 16, lanes[0]), F32)
        scratch[f"qs{i}"] = pltpu.VMEM((16, lanes[0]), F32)
    scratch["gsend"] = pltpu.SemaphoreType.DMA((3, 3, max(sizes)))
    scratch["grecv"] = pltpu.SemaphoreType.DMA((3, 3, max(sizes)))

    names = list(scratch)

    def kernel(rs_ref, sg_ref, re_ref, sol_ref, res_ref, *refs):
        R = dict(zip(names, refs))
        pos = [lax.axis_index(a) for a in AXES]

        def zero(ref):
            ref[...] = jnp.zeros(ref.shape, F32)

        for k in range(LEVELS):
            X, Y, Z = shapes[k]
            for b in range(R[f"e{k}"].shape[0]):
                zero(R[f"e{k}"].at[b, 0])
                zero(R[f"e{k}"].at[b, X + 1])
                if k >= LOCAL:
                    Yp = up_to(Y, 8)
                    for x in range(1, X + 1):
                        R[f"e{k}"][b, x, 0:8, :] = jnp.zeros((8, lanes[k]), F32)
                        R[f"e{k}"][b, x, Yp + 8 :, :] = jnp.zeros((8, lanes[k]), F32)
                else:
                    zero(R[f"zr{k}"].at[b, 0])
                    zero(R[f"zr{k}"].at[b, 1])
                    zero(R[f"yr{k}"].at[b, 0])
                    zero(R[f"yr{k}"].at[b, 1])
            if k < LEVELS - 1 and Y // 2 % 8:
                for m in range(lanes[k] // 128):
                    for x in range(X // 2):
                        R[f"t{k}"][m, x, Y:, :] = jnp.zeros((R[f"t{k}"].shape[2] - Y, 128), F32)

        barrier = pltpu.get_barrier_semaphore()
        for axis, n, me in zip(AXES, sizes, pos):
            for d in range(1, n):
                pl.semaphore_signal(barrier, inc=1, device_id={axis: lax.rem(me + d, n)}, device_id_type=MESH)
        pl.semaphore_wait(barrier, sum(n - 1 for n in sizes))

        pending = []

        def copies(k, b):
            X, Y, Z = shapes[k]
            e = R[f"e{k}"]
            zs, zr, ys, yr = (R[f"{m}{k}"] for m in ("zs", "zr", "ys", "yr"))
            out = []
            pairs = (
                (e.at[b, 1, pl.ds(8, Y), :], e.at[b, X + 1, pl.ds(8, Y), :]),
                (e.at[b, X, pl.ds(8, Y), :], e.at[b, 0, pl.ds(8, Y), :]),
                (ys.at[b, 0], yr.at[b, 1]),
                (ys.at[b, 1], yr.at[b, 0]),
                (zs.at[b, 0], zr.at[b, 1]),
                (zs.at[b, 1], zr.at[b, 0]),
            )
            for i, (src, dst) in enumerate(pairs):
                axis, me, n = AXES[i // 2], pos[i // 2], sizes[i // 2]
                target = me - 1 if i % 2 == 0 else me + 1
                low, high = me > 0, me < n - 1
                copy = pltpu.make_async_remote_copy(
                    src_ref=src,
                    dst_ref=dst,
                    send_sem=R[f"send{k}"].at[b, i],
                    recv_sem=R[f"recv{k}"].at[b, i],
                    device_id={axis: target},
                    device_id_type=MESH,
                )
                out.append((copy, low if i % 2 == 0 else high, high if i % 2 == 0 else low))
            return out

        def send(k, b):
            for copy, sends, _ in copies(k, b):
                pl.when(sends)(copy.start)
            pending.append((k, b))

        def receive(k, b):
            X, Y, Z = shapes[k]
            for copy, _, receives in copies(k, b):
                pl.when(receives)(copy.wait_recv)
            for x in range(X):
                R[f"e{k}"][b, x + 1, 7:8, :] = R[f"yr{k}"][b, 0, x : x + 1, :]
                R[f"e{k}"][b, x + 1, 8 + Y : 9 + Y, :] = R[f"yr{k}"][b, 1, x : x + 1, :]

        def applied(k, b, x, split):
            X, Y, Z = shapes[k]
            L = lanes[k]
            Yp = up_to(Y, 8)
            e = R[f"e{k}"]
            i = x + 1
            c = e[b, i, 8 : 8 + Yp, :]
            beside = e[b, i + 1, 8 : 8 + Yp, :] + e[b, i - 1, 8 : 8 + Yp, :]
            beside = beside + (e[b, i, 9 : 9 + Yp, :] + e[b, i, 7 : 7 + Yp, :])
            beside = beside + (pltpu.roll(c, 1, 1) + pltpu.roll(c, L - 1, 1))
            if split:
                lane = lane_of(Yp, L)
                low = pltpu.roll(R[f"zr{k}"][b, 0], lax.rem(L - x, L), 1)
                high = pltpu.roll(R[f"zr{k}"][b, 1], lax.rem(L + Z - 1 - x, L), 1)
                beside = beside + jnp.where(lane == 0, low, jnp.where(lane == Z - 1, high, 0.0))
            return c, 0.25**k * (6.0 * c - beside) + R[f"s{k}"][x] * c

        def produce(k, b, f):
            X, Y, Z = shapes[k]
            L = lanes[k]
            lane = lane_of(Y, L)

            def one(x, faces):
                low, high = faces
                v = f(x)
                R[f"e{k}"][b, x + 1, 8 : 8 + Y, :] = v
                R[f"ys{k}"][b, 0, pl.ds(x, 1), :] = v[0:1]
                R[f"ys{k}"][b, 1, pl.ds(x, 1), :] = v[Y - 1 : Y]
                low = jnp.where(lane == x, pltpu.roll(v, x, 1), low)
                high = jnp.where(lane == x, pltpu.roll(v, lax.rem(x + L - Z + 1, L), 1), high)
                return low, high

            low, high = loop(X, one, (jnp.zeros((Y, L), F32), jnp.zeros((Y, L), F32)))
            R[f"zs{k}"][b, 0] = low
            R[f"zs{k}"][b, 1] = high
            send(k, b)

        def relaxed(k, b, x, split):
            c, a = applied(k, b, x, split)
            return c + R[f"w{k}"][x] * (R[f"f{k}"][x] - a)

        def keep(k, j, n, v):
            for m in range(lanes[k] // 128):
                R[f"t{k}"][m, j, 0:n, :] = v[:, 128 * m : 128 * m + 128]

        def kept(k, j, n):
            v = [R[f"t{k}"][m, j, 0:n, :] for m in range(lanes[k] // 128)]
            return v[0] if len(v) == 1 else jnp.concatenate(v, axis=1)

        def double_rows(k, v):
            n = v.shape[1]
            for m in range(lanes[k] // 128):
                for d in range(2):
                    R[f"t{k}"][m, :, pl.ds(d, n, stride=2), :] = v[:, :, 128 * m : 128 * m + 128]

        def pairs_of(k, f):
            X, Y, Z = shapes[k]

            def one(j, c):
                keep(k, j, up_to(Y, 8), f(2 * j) + f(2 * j + 1))
                return c

            loop(X // 2, one, 0, 2)

        def halve_rows(k):
            t = R[f"t{k}"]
            n = t.shape[2] // 2
            v = [
                t[m, :, pl.ds(0, n, stride=2), :] + t[m, :, pl.ds(1, n, stride=2), :]
                for m in range(lanes[k] // 128)
            ]
            v = [u.reshape(u.shape[0] * n, 128) for u in v]
            return v[0] if len(v) == 1 else jnp.concatenate(v, axis=1)

        def coarsened(k):
            X, Y, Z = shapes[k]
            n = R[f"t{k}"].shape[2] // 2
            C = pick(lanes[k], lanes[k + 1], lambda r, c: (r // 2 == c) & (r < Z), 0.125)
            return dot(halve_rows(k), C).reshape(X // 2, n, lanes[k + 1])

        def weights(k):
            X, Y, Z = shapes[k]
            Yp = up_to(Y, 8)
            lane = lane_of(Yp, lanes[k])

            def one(x, c):
                s = jnp.where(lane < Z, R[f"s{k}"][x], 0.0)
                R[f"w{k}"][x] = jnp.where(lane < Z, damping / (6.0 * 0.25**k + s), 0.0)
                return c

            loop(X, one)

        def spread(g, stage):
            axis_at = 2 - stage
            axis, n, me = AXES[axis_at], sizes[axis_at], pos[axis_at]
            if stage == 0:
                src, dst = R[f"gz{g}"].at[me], R[f"gz{g}"].at[me]
            elif stage == 1:
                here = pl.ds(pl.multiple_of(me * rows, 8), rows)
                src, dst = R[f"gm{g}"], R[f"gy{g}"].at[:, here, :]
            else:
                src, dst = R[f"gy{g}"], R[f"gx{g}"].at[me]
            return [
                pltpu.make_async_remote_copy(
                    src_ref=src,
                    dst_ref=dst,
                    send_sem=R["gsend"].at[g, stage, d],
                    recv_sem=R["grecv"].at[g, stage, d],
                    device_id={axis: lax.rem(me + d, n)},
                    device_id_type=MESH,
                )
                for d in range(1, n)
            ]

        def gather_first(g):
            k = LOCAL - 1
            Z = shapes[k][2]
            v = halve_rows(k)
            v = v.reshape(packs, slabs * rows, v.shape[1])
            block_sum = None
            for h in range(packs):
                at = pos[2] * part[2] + h * half
                C = pick(lanes[k], glanes, lambda r, c: (r // 2 + at == c) & (r < Z), 0.125)
                piece = dot(v[h], C)
                block_sum = piece if block_sum is None else block_sum + piece
            R[f"gz{g}"][pos[2]] = block_sum.reshape(slabs, rows, glanes)
            for copy in spread(g, 0):
                copy.start()

        def gather_second(g):
            for copy in spread(g, 0):
                copy.wait_recv()
            v = R[f"gz{g}"][0]
            for i in range(1, nz):
                v = v + R[f"gz{g}"][i]
            R[f"gm{g}"][...] = v
            for copy in spread(g, 1):
                copy.start()
            R[f"gy{g}"][:, pl.ds(pl.multiple_of(pos[1] * rows, 8), rows), :] = v

        def gather_third(g):
            for copy in spread(g, 1):
                copy.wait_recv()
            for copy in spread(g, 2):
                copy.start()

        def gather_last(g, name):
            k = LOCAL
            lane = lane_of(part[1], glanes)
            R[f"gx{g}"][pos[0]] = R[f"gy{g}"][...]
            for copy in spread(g, 2):
                copy.wait_recv()
            for i in range(nx):
                for h in range(packs):
                    for j in range(slabs):
                        x = (i * packs + h) * slabs + j
                        for m in range(ny):
                            v = R[f"gx{g}"][i, j, m * rows : m * rows + part[1], :]
                            if h:
                                v = pltpu.roll(v, glanes - h * half, 1)
                            if packs > 1:
                                v = jnp.where(lane < wide, v, 0.0)
                            R[f"{name}{k}"][x, m * part[1] : (m + 1) * part[1], :] = v

        def gather_sends(g):
            for stage in range(3):
                for copy in spread(g, stage):
                    copy.wait_send()

        X, Y, Z = block
        L = lanes[0]

        def fill_guess(x):
            v = sg_ref[x]
            return jnp.concatenate([v, jnp.zeros((Y, L - Z), F32)], axis=1)

        produce(0, 0, fill_guess)

        def fill(x, c):
            v = jnp.concatenate([re_ref[x], jnp.zeros((Y, L - Z), F32)], axis=1)
            R["s0"][x] = v
            return c

        loop(X, fill)
        weights(0)
        for k in range(LOCAL):
            pairs_of(k, lambda x: R[f"s{k}"][x])
            if k < LOCAL - 1:
                R[f"s{k + 1}"][...] = coarsened(k)
                weights(k + 1)
            else:
                gather_first(0)

        receive(0, 0)

        def residual_of(x):
            c, a = applied(0, 0, x, True)
            f = jnp.concatenate([rs_ref[x], jnp.zeros((Y, L - Z), F32)], axis=1) - a
            R["f0"][x] = f
            return R["w0"][x] * f

        produce(0, 1, residual_of)
        gather_second(0)
        receive(0, 1)
        produce(0, 2, lambda x: relaxed(0, 1, x, True))
        gather_third(0)

        def left(k, b, x, split):
            c, a = applied(k, b, x, split)
            return R[f"f{k}"][x] - a

        receive(0, 2)
        pairs_of(0, lambda x: left(0, 2, x, True))
        R["f1"][...] = coarsened(0)
        produce(1, 0, lambda x: R["w1"][x] * R["f1"][x])
        gather_last(0, "s")
        for k in range(LOCAL, LEVELS):
            weights(k)
            if k < LEVELS - 1:
                pairs_of(k, lambda x: R[f"s{k}"][x])
                R[f"s{k + 1}"][...] = coarsened(k)
        receive(1, 0)
        produce(1, 1, lambda x: relaxed(1, 0, x, True))
        receive(1, 1)
        pairs_of(1, lambda x: left(1, 1, x, True))
        gather_first(1)
        gather_second(1)
        gather_third(1)
        gather_last(1, "f")

        def solve(k):
            X, Y, Z = shapes[k]
            Yp, L = up_to(Y, 8), lanes[k]
            e, f, w = R[f"e{k}"], R[f"f{k}"], R[f"w{k}"]

            def put(b, g):
                def one(x, c):
                    e[b, x + 1, 8 : 8 + Yp, :] = g(x)
                    return c

                loop(X, one)

            if k == LEVELS - 1:
                inside = (lane_of(Yp, L) < Z) & (lax.broadcasted_iota(jnp.int32, (Yp, L), 0) < Y)
                r = [jnp.where(inside, f[x], 0.0) for x in range(X)]
                p = list(r)
                answer = [jnp.zeros((Yp, L), F32) for _ in range(X)]

                def inner(u, v):
                    s = u[0] * v[0]
                    for x in range(1, X):
                        s = s + u[x] * v[x]
                    return total(s)

                rr = inner(r, r)
                for _ in range(BOTTOM_ITERS):
                    for x in range(X):
                        e[0, x + 1, 8 : 8 + Yp, :] = p[x]
                    q = [jnp.where(inside, applied(k, 0, x, False)[1], 0.0) for x in range(X)]
                    a = rr / inner(p, q)
                    answer = [u + a * v for u, v in zip(answer, p)]
                    r = [u - a * v for u, v in zip(r, q)]
                    new = inner(r, r)
                    ratio = new / rr
                    p = [u + ratio * v for u, v in zip(r, p)]
                    rr = new
                for x in range(X):
                    e[1, x + 1, 8 : 8 + Yp, :] = answer[x]
                return
            put(0, lambda x: w[x] * f[x])
            put(1, lambda x: relaxed(k, 0, x, False))
            pairs_of(k, lambda x: left(k, 1, x, False))
            R[f"f{k + 1}"][...] = coarsened(k)
            solve(k + 1)
            prolong(k)
            put(0, lambda x: e[1, x + 1, 8 : 8 + Yp, :] + kept(k, x // 2, Yp))
            put(1, lambda x: relaxed(k, 0, x, False))
            put(0, lambda x: relaxed(k, 1, x, False))

        def prolong(k):
            X, Y, Z = shapes[k]
            Yc = up_to(Y // 2, 8)
            b = 1 if k + 1 == LEVELS - 1 else 0
            C = pick(lanes[k + 1], lanes[k], lambda r, c: (c // 2 == r) & (c < Z), 1.0)
            v = R[f"e{k + 1}"][b, 1 : X // 2 + 1, 8 : 8 + Yc, :]
            v = dot(v.reshape(X // 2 * Yc, lanes[k + 1]), C).reshape(X // 2, Yc, lanes[k])
            double_rows(k, v)

        solve(LOCAL)

        k = LOCAL - 1
        Xk, Yk, Zk = shapes[k]
        C = pick(glanes, lanes[k], lambda r, c: (c // 2 + pos[2] * part[2] == r) & (c < Zk), 1.0)
        B = pick(Yk, shapes[LOCAL][1], lambda r, c: r // 2 + pos[1] * part[1] == c, 1.0)
        for j in range(Xk // 2):
            v = R[f"e{LOCAL}"][0, pos[0] * part[0] + j + 1, 8 : 8 + shapes[LOCAL][1], :]
            keep(k, j, Yk, dot(dot(B, v), C))
        produce(1, 2, lambda x: R["e1"][1, x + 1, 8 : 8 + Yk, :] + kept(1, x // 2, Yk))
        receive(1, 2)
        produce(1, 3, lambda x: relaxed(1, 2, x, True))
        receive(1, 3)

        def last_one(x, c):
            v = relaxed(1, 3, x, True)
            R["w1"][x] = v
            return c

        loop(Xk, last_one)
        C = pick(lanes[1], lanes[0], lambda r, c: (c // 2 == r) & (c < Z), 1.0)
        v = dot(R["w1"][...].reshape(Xk * Yk, lanes[1]), C).reshape(Xk, Yk, lanes[0])
        double_rows(0, v)
        produce(0, 3, lambda x: R["e0"][2, x + 1, 8 : 8 + Y, :] + kept(0, x // 2, Y))
        receive(0, 3)
        produce(0, 4, lambda x: relaxed(0, 3, x, True))
        receive(0, 4)
        produce(0, 5, lambda x: relaxed(0, 4, x, True))
        receive(0, 5)

        def image(x, sums):
            upper, lower = sums
            c, a = applied(0, 5, x, True)
            R["ap"][x] = a
            return upper + fold(R["f0"][x] * c), lower + fold(a * c)

        upper, lower = loop(X, image, (jnp.zeros((8, L), F32), jnp.zeros((8, L), F32)))
        for i in range(3):
            n, me = sizes[i], pos[i]
            R[f"qs{i}"][0:8] = upper
            R[f"qs{i}"][8:16] = lower
            sums = [
                pltpu.make_async_remote_copy(
                    src_ref=R[f"qs{i}"],
                    dst_ref=R[f"q{i}"].at[me],
                    send_sem=R["gsend"].at[2, i, d],
                    recv_sem=R["grecv"].at[2, i, d],
                    device_id={AXES[i]: lax.rem(me + d, n)},
                    device_id_type=MESH,
                )
                for d in range(1, n)
            ]
            for copy in sums:
                copy.start()
            R[f"q{i}"][me] = R[f"qs{i}"][...]
            for copy in sums:
                copy.wait_recv()
            v = R[f"q{i}"][0]
            for d in range(1, n):
                v = v + R[f"q{i}"][d]
            upper, lower = v[0:8], v[8:16]
            for copy in sums:
                copy.wait_send()
        step_length = total(upper) / total(lower)

        def finish(x, c):
            p = R["e0"][5, x + 1, 8 : 8 + Y, :]
            sol_ref[x] = sg_ref[x] + (step_length * p)[:, 0:Z]
            res_ref[x] = (R["f0"][x] - step_length * R["ap"][x])[:, 0:Z]
            return c

        loop(X, finish)
        for k, b in pending:
            for copy, sends, _ in copies(k, b):
                pl.when(sends)(copy.wait_send)
        gather_sends(0)
        gather_sends(1)

    return kernel, list(scratch.values())


def solution(mesh):
    sizes = tuple(mesh.shape[a] for a in AXES)

    def body(right_side, start_guess, reaction):
        kernel, scratch = make_kernel(sizes, right_side.shape)
        out = jax.ShapeDtypeStruct(right_side.shape, F32)
        return tuple(
            pl.pallas_call(
                kernel,
                out_shape=(out, out),
                in_specs=[pl.BlockSpec(memory_space=pltpu.VMEM)] * 3,
                out_specs=(pl.BlockSpec(memory_space=pltpu.VMEM),) * 2,
                scratch_shapes=scratch,
                compiler_params=pltpu.CompilerParams(
                    collective_id=0, has_side_effects=True, vmem_limit_bytes=60 * 2**20
                ),
                name="cg_step",
            )(right_side, start_guess, reaction)
        )

    placed = P(*AXES)
    return jax.shard_map(
        body, mesh=mesh, in_specs=(placed,) * 3, out_specs=(placed,) * 2, check_vma=False
    )
```
